32 devices in a mesh: row: 8 (over z, x), col: 4 (over y, core).
Axes of the slice: x: 2, y: 2, z: 4, core: 2. Of those that a mesh axis runs over, the one named last changes fastest.
Arguments:
- features: bfloat16 [32768, 256], P(('col', 'row')), may hold values from -6 to 6
- adjacency: bfloat16 [256, 4, 12, 128, 128], P('row', 'col'), may hold values from 0 to 0.023925781
- block_cols: int32 [256, 4, 12], P('row', 'col'), may hold values from 0 to 63, as said below
- block_live: int32 [256, 4], P('row', 'col'), may hold values from 1 to 12, as said below
- weight: bfloat16 [256, 256], replicated, may hold values from -0.375 to 0.375
- bias: float32 [256], replicated, may hold values from -3 to 3
- upstream: bfloat16 [32768, 256], P(('row', 'col')), may hold values from -6 to 6
Outputs:
- activations: bfloat16 [32768, 256], P(('row', 'col'))
- feature_grad: bfloat16 [32768, 256], P(('col', 'row'))
- weight_grad: float32 [256, 256], replicated
- bias_grad: float32 [256], replicated
The draws below stay inside these ranges and needn't reach their ends.
Inputs may be any that keep to these rules, and one draw needn't show every extreme that they name: `block_cols`: the live slots of one block row in one column tile name distinct column blocks of that tile. Slots k with k < block_live[i, c] are live; the other slots of block_cols and adjacency are ignored. Some entry equals 12.
All inputs are finite; a program needn't handle non-finite values.
Results may differ from the reference program's by a relative error of at most 0.014.
Values may be sent and summed in bfloat16 or wider, within the bound.
No kernel may reach another device: no remote copies, remote signals or barrier semaphores. Data moves between devices by JAX's collectives and lax.ppermute only.
A program may use at most 256 MiB of HBM per device.

```python
import jax
import jax.numpy as jnp
from jax import lax

F = 256
BS = 128
BR = 32
KB = 12
NBR = 256
BCOL = 64
N = 32768
N_ROW = 8
N_COL = 4


def draw_block_cols(key, part):
    tile_blocks = BR * N_ROW // N_COL
    scores = jax.random.randint(key, (BR * N_ROW, N_COL, tile_blocks), 0, 1 << 20) * tile_blocks
    scores = scores + jnp.arange(tile_blocks, dtype=jnp.int32)
    ranked = jnp.argsort(scores, axis=-1)
    return ranked[:, :, :KB].astype(jnp.int32)


def draw_block_live(key, part):
    heavy_key = jax.random.fold_in(key, 11)
    base_key = jax.random.fold_in(key, 12)
    place_key = jax.random.fold_in(key, 13)
    heavy_factor = jax.random.randint(heavy_key, (N_ROW, 1, N_COL), 0, 4)
    base_count = jax.random.randint(base_key, (N_ROW, BR, N_COL), 1, max(KB // 4, 1) + 1)
    live_count = jnp.minimum(base_count * (1 + heavy_factor), KB).reshape(-1)
    position = jax.random.randint(place_key, (), 0, BR * N_ROW * N_COL)
    live_count = live_count.at[position].set(KB)
    return live_count.reshape(BR * N_ROW, N_COL).astype(jnp.int32)


def shard_levels(key, shape, pieces, low, top_value):
    level, own = 1.0, jax.random.fold_in(key, 6)
    for dim, blocks in pieces:
        heights = jnp.exp(jax.random.uniform(jax.random.fold_in(own, dim), (blocks,), jnp.float32, low / len(pieces), top_value / len(pieces)))
        level = level * jnp.repeat(heights, shape[dim] // blocks).reshape([-1 if axis == dim else 1 for axis in range(len(shape))])
    return level


def noise(own_key, extent, deviation, reach, split=(), kind=jnp.bfloat16):
    entries = deviation * jax.random.normal(own_key, extent, jnp.float32)
    if split:
        entries = entries * shard_levels(own_key, extent, split, -0.22, 0.18)
    return jnp.clip(entries, -reach, reach).astype(kind)


def setup_inputs(seed: int = 0) -> dict:
    keys = jax.random.split(jax.random.key(seed), 8)
    return {
        "features": noise(keys[0], (N, F), 1.0, 6.0, ((0, 32),)),
        "adjacency": jnp.clip(0.023925781 * jax.random.uniform(keys[1], (NBR, N_COL, KB, BS, BS), jnp.float32) ** shard_levels(keys[1], (NBR, N_COL, KB, BS, BS), ((0, 8), (1, 4)), -0.2, 0.2), 0.0, 0.023925781).astype(jnp.bfloat16),
        "block_cols": draw_block_cols(jax.random.fold_in(keys[7], 71), 0),
        "block_live": draw_block_live(jax.random.fold_in(keys[7], 71), 0),
        "weight": noise(keys[4], (F, F), F ** -0.5, 0.375),
        "bias": noise(keys[5], (F,), 0.5, 3.0, (), jnp.float32),
        "upstream": noise(keys[6], (N, F), 1.0, 6.0, ((0, 32),)),
    }


def reference(features, adjacency, block_cols, block_live, weight, bias, upstream):
    panels = features.reshape(N_COL, BCOL, BS, F)
    slot_ids = jnp.arange(KB)
    tile_ids = jnp.arange(N_COL)[:, None]

    def row_product(inputs):
        blocks, column_ids, live_count = inputs
        picked = panels[tile_ids, column_ids].astype(jnp.float32)
        live_mask = slot_ids[None, :] < live_count[:, None]
        picked = jnp.where(live_mask[:, :, None, None], picked, jnp.float32(0.0))
        return jnp.einsum("ckab,ckbf->af", blocks.astype(jnp.float32), picked)

    aggregated = lax.map(row_product, (adjacency, block_cols, block_live))
    aggregated = aggregated.reshape(N, F).astype(jnp.bfloat16)
    preact = jnp.dot(aggregated, weight, preferred_element_type=jnp.float32) + bias
    sigmoid_pre = jax.nn.sigmoid(preact)
    activations = (preact * sigmoid_pre).astype(jnp.bfloat16)
    derivative = sigmoid_pre * (1.0 + preact * (1.0 - sigmoid_pre))
    grad_pre = (upstream.astype(jnp.float32) * derivative).astype(jnp.bfloat16)
    weight_grad = jnp.dot(aggregated.T, grad_pre, preferred_element_type=jnp.float32)
    bias_grad = jnp.sum(grad_pre.astype(jnp.float32), axis=0)
    grad_agg = jnp.dot(grad_pre, weight.T, preferred_element_type=jnp.float32).astype(jnp.bfloat16)
    grad_blocks = grad_agg.reshape(NBR, BS, F)

    def spread(totals, inputs):
        blocks, column_ids, live_count, grad_rows = inputs
        contrib = jnp.einsum("ckab,af->ckbf", blocks.astype(jnp.float32), grad_rows.astype(jnp.float32))
        live_mask = slot_ids[None, :] < live_count[:, None]
        contrib = jnp.where(live_mask[:, :, None, None], contrib, jnp.float32(0.0))
        totals = totals.at[tile_ids, column_ids].add(contrib)
        return totals, None

    totals = jnp.zeros((N_COL, BCOL, BS, F), jnp.float32)
    totals, _ = lax.scan(spread, totals, (adjacency, block_cols, block_live, grad_blocks))
    feature_grad = totals.reshape(N, F).astype(jnp.bfloat16)
    return activations, feature_grad, weight_grad, bias_grad
```

```python
import functools

import jax
import jax.numpy as jnp
from jax import lax
from jax.experimental import pallas as pl
from jax.experimental.pallas import tpu as pltpu
from jax.sharding import PartitionSpec as P


F32 = jnp.float32
BF16 = jnp.bfloat16
I32 = jnp.int32
GROUP = 4


def split_row(n_row):
    nx = 1
    while (2 * nx) ** 2 <= n_row and n_row % (2 * nx) == 0:
        nx *= 2
    return n_row // nx, nx


def split_col(n_col):
    nc = 2 if n_col % 2 == 0 else 1
    return n_col // nc, nc


def shift_major(major, minor, step):
    return [
        (a * minor + b, ((a + step) % major) * minor + b)
        for a in range(major)
        for b in range(minor)
    ]


def shift_minor(major, minor, step):
    return [
        (a * minor + b, a * minor + (b + step) % minor)
        for a in range(major)
        for b in range(minor)
    ]


def as_blocks(ref, bs):
    value = ref[...]
    return value.reshape(value.shape[0] // bs, bs, value.shape[1])


def fill_panel(panel, pieces, bs):
    at = 0
    for piece in pieces:
        blocks = as_blocks(piece, bs)
        panel[at : at + blocks.shape[0]] = blocks
        at += blocks.shape[0]
    panel[at] = jnp.zeros(panel.shape[1:], panel.dtype)


def block_rows_at(index, bs):
    return pl.ds(pl.multiple_of(index * bs, bs), bs)


def early_kernel(slots, n_pieces, rows_ref, index_ref, mats, *refs):
    pieces = refs[:n_pieces]
    away_ref, kept_ref, panel = refs[n_pieces:]
    bs = mats.shape[-1]
    fill_panel(panel, pieces, bs)
    half = away_ref.shape[0] // bs
    for part, out_ref in enumerate((away_ref, kept_ref)):

        @pl.loop(0, half // 2)
        def _(pair, part=part, out_ref=out_ref):
            for r in range(2):
                at = pair * 2 + r
                row = rows_ref[part * half + at]
                first = row * slots
                lhs = [mats[first + k] for k in range(slots)]
                rhs = [panel[index_ref[first + k]] for k in range(slots)]
                out_ref[block_rows_at(at, bs), :] = jnp.dot(
                    jnp.concatenate(lhs, axis=1),
                    jnp.concatenate(rhs, axis=0),
                    preferred_element_type=F32,
                )


def cost(flops, moved):
    return pl.CostEstimate(flops=flops, bytes_accessed=moved, transcendentals=0)


SMEM_SPEC = pl.BlockSpec(memory_space=pltpu.SMEM)
VMEM_SPEC = pl.BlockSpec(memory_space=pltpu.VMEM)


def early_product(mats, pieces, rows, index, slots):
    n_mats, bs, _ = mats.shape
    n_rows = n_mats // slots
    width = pieces[0].shape[1]
    bps = pieces[0].shape[0] // bs
    out = jax.ShapeDtypeStruct((n_rows // 2 * bs, width), F32)
    return pl.pallas_call(
        functools.partial(early_kernel, slots, len(pieces)),
        name="early",
        out_shape=(out, out),
        in_specs=[SMEM_SPEC] * 2 + [VMEM_SPEC] * (1 + len(pieces)),
        out_specs=(VMEM_SPEC, VMEM_SPEC),
        scratch_shapes=[pltpu.VMEM((len(pieces) * bps + 1, bs, width), BF16)],
        compiler_params=pltpu.CompilerParams(vmem_limit_bytes=24 << 20),
        cost_estimate=cost(2 * n_mats * bs * bs * width, 20 << 20),
    )(rows, index, mats, *pieces)


def late_kernel(slots, part, rows_ref, count_ref, entry_ref, source_ref, mats, piece, acc_ref, out_ref, panel):
    bs = mats.shape[-1]
    fill_panel(panel, [piece], bs)
    half = out_ref.shape[0] // bs

    def term(row, g):
        at = row * (slots + 2) + 2 * g
        lhs = [mats[entry_ref[at + k]] for k in range(2)]
        rhs = [panel[source_ref[at + k]] for k in range(2)]
        return jnp.dot(
            jnp.concatenate(lhs, axis=1),
            jnp.concatenate(rhs, axis=0),
            preferred_element_type=F32,
        )

    @pl.loop(0, half // 2)
    def _(pair):
        places = [pair * 2 + r for r in range(2)]
        rows = [rows_ref[part * half + at] for at in places]
        accs = tuple(
            acc_ref[block_rows_at(at, bs), :] + term(row, 0)
            for at, row in zip(places, rows, strict=True)
        )
        for r in range(2):

            def more(g, acc, r=r):
                return acc + term(rows[r], g)

            acc = lax.fori_loop(1, (count_ref[rows[r]] + 1) // 2, more, accs[r])
            out_ref[block_rows_at(places[r], bs), :] = acc.astype(BF16)


def late_product(mats, piece, acc, rows, count, entry, source, slots, part):
    bs = mats.shape[1]
    width = piece.shape[1]
    bps = piece.shape[0] // bs
    return pl.pallas_call(
        functools.partial(late_kernel, slots, part),
        name="late",
        out_shape=jax.ShapeDtypeStruct(acc.shape, BF16),
        in_specs=[SMEM_SPEC] * 4 + [VMEM_SPEC] * 3,
        out_specs=VMEM_SPEC,
        scratch_shapes=[pltpu.VMEM((bps + 1, bs, width), BF16)],
        compiler_params=pltpu.CompilerParams(vmem_limit_bytes=20 << 20),
        cost_estimate=cost(acc.size * bs, 4 << 20),
    )(rows, count, entry, source, mats, piece, acc)


def lists_kernel(
    slots, n_rows, n_blocks, n_list, late_from, bps,
    cols_ref, live_ref, place_ref,
    count_ref, entry_ref, source_ref, late_count_ref, late_entry_ref, late_source_ref,
):
    @pl.loop(0, n_blocks)
    def _(b):
        count_ref[b] = 0

    @pl.loop(0, n_rows)
    def _(row):
        place = place_ref[row]

        def visit(k, late):
            at = row * slots + k
            b = cols_ref[at]
            n = count_ref[b]
            entry_ref[b * n_list + n] = at
            source_ref[b * n_list + n] = place
            count_ref[b] = n + 1
            late_entry_ref[row * (slots + 2) + late] = at
            late_source_ref[row * (slots + 2) + late] = jnp.maximum(b - late_from, 0)
            return late + (b >= late_from).astype(I32)

        late = lax.fori_loop(0, live_ref[row], visit, jnp.int32(0))
        late_count_ref[row] = late
        for k in range(2):
            late_entry_ref[row * (slots + 2) + late + k] = row * slots
            late_source_ref[row * (slots + 2) + late + k] = bps

    @pl.loop(0, n_blocks)
    def _(b):
        n = count_ref[b]
        for k in range(GROUP):
            entry_ref[b * n_list + n + k] = 0
            source_ref[b * n_list + n + k] = n_rows


def slot_lists(cols, live, place, slots, n_blocks, late_from, bps):
    n_rows = live.shape[0]
    n_list = n_rows + GROUP
    sizes = (n_blocks, n_blocks * n_list, n_blocks * n_list, n_rows, n_rows * (slots + 2), n_rows * (slots + 2))
    return pl.pallas_call(
        functools.partial(lists_kernel, slots, n_rows, n_blocks, n_list, late_from, bps),
        name="lists",
        out_shape=tuple(jax.ShapeDtypeStruct((size,), I32) for size in sizes),
        in_specs=[SMEM_SPEC] * 3,
        out_specs=(SMEM_SPEC,) * 6,
        cost_estimate=cost(0, 20 << 20),
    )(cols, live, place)


def backward_kernel(n_list, n_pieces, firsts, bps, count_ref, entry_ref, source_ref, mats, *refs):
    pieces = refs[:n_pieces]
    outs, panel = refs[n_pieces:-1], refs[-1]
    bs = mats.shape[-1]
    fill_panel(panel, pieces, bs)

    def term(b, g):
        at = b * n_list + jnp.minimum(g * GROUP, count_ref[b])
        lhs = [mats[entry_ref[at + k]] for k in range(GROUP)]
        rhs = [panel[source_ref[at + k]] for k in range(GROUP)]
        return lax.dot_general(
            jnp.concatenate(lhs, axis=0),
            jnp.concatenate(rhs, axis=0),
            (((0,), (0,)), ((), ())),
            preferred_element_type=F32,
        )

    for first, out_ref in zip(firsts, outs, strict=True):

        @pl.loop(0, bps // 2)
        def _(pair, first=first, out_ref=out_ref):
            here = [first + 2 * pair + r for r in range(2)]
            most = jnp.maximum(count_ref[here[0]], count_ref[here[1]])
            accs = tuple(term(b, 0) for b in here)

            def more(g, accs):
                return tuple(acc + term(b, g) for b, acc in zip(here, accs, strict=True))

            accs = lax.fori_loop(1, (most + GROUP - 1) // GROUP, more, accs)
            for r in range(2):
                out_ref[block_rows_at(2 * pair + r, bs), :] = accs[r].astype(BF16)


def backward_product(mats, pieces, lists, firsts, bps, slots):
    count, entry, source = lists
    n_mats, bs, _ = mats.shape
    n_rows = n_mats // slots
    width = pieces[0].shape[1]
    out = jax.ShapeDtypeStruct((bps * bs, width), BF16)
    share = n_mats // 8 * len(firsts)
    return pl.pallas_call(
        functools.partial(backward_kernel, n_rows + GROUP, len(pieces), firsts, bps),
        name="backward",
        out_shape=(out,) * len(firsts),
        in_specs=[SMEM_SPEC] * 3 + [VMEM_SPEC] * (1 + len(pieces)),
        out_specs=(VMEM_SPEC,) * len(firsts),
        scratch_shapes=[pltpu.VMEM((n_rows + 1, bs, width), BF16)],
        compiler_params=pltpu.CompilerParams(vmem_limit_bytes=20 << 20),
        cost_estimate=cost(2 * share * bs * bs * width, 4 << 20),
    )(count, entry, source, mats, *pieces)


def local(n_row, n_col, features, adjacency, block_cols, block_live, weight, bias, upstream):
    n_rows, _, slots, bs, _ = adjacency.shape
    width = features.shape[1]
    nz, nx = split_row(n_row)
    ny, nc = split_col(n_col)
    bps = features.shape[0] // bs
    rpc = n_rows // n_col
    me_row, me_col = lax.axis_index("row"), lax.axis_index("col")
    z, x = me_row // nx, me_row % nx
    y, c = me_col // nc, me_col % nc
    to_z = shift_major(nz, nx, 1)
    to_x = shift_minor(nz, nx, 1)
    to_y = shift_major(ny, nc, 1)
    to_c = shift_minor(ny, nc, 1)

    live = block_live.reshape(n_rows)
    cols = block_cols.reshape(n_rows, slots)
    shard = cols // bps
    back_z = (z - shard // nx) % nz
    back_x = (x - shard % nx) % nx
    cols = (back_z * nx + back_x) * bps + cols % bps
    late_from = (n_row - 1) * bps
    is_live = lax.broadcasted_iota(I32, (n_rows, slots), 1) < live[:, None]
    index = jnp.where(is_live, jnp.minimum(cols, late_from), late_from).reshape(-1)
    cols = cols.reshape(-1)
    row_ids = jnp.arange(n_rows, dtype=I32)
    owner = row_ids // rpc
    back_y = (y - owner // nc) % ny
    back_c = (c - owner % nc) % nc
    place = ((back_y * nc + back_c) * rpc + row_ids % rpc).astype(I32)
    order = [(v, u) for u in list(range(1, nc)) + [0] for v in list(range(1, ny)) + [0]]
    dest = jnp.stack([((y - v) % ny) * nc + (c - u) % nc for v, u in order])
    rows = (dest[:, None] * rpc + jnp.arange(rpc, dtype=I32)[None, :]).reshape(-1).astype(I32)
    mats = pltpu.with_memory_space_constraint(
        adjacency.reshape(n_rows * slots, bs, bs), pltpu.VMEM
    )

    pieces = []
    moving = features
    for j in range(nz):
        across = moving
        pieces.append(across)
        for _ in range(1, nx):
            across = lax.ppermute(across, "row", to_x)
            pieces.append(across)
        if j < nz - 1:
            moving = lax.ppermute(moving, "row", to_z)
    *lists, late_count, late_entry, late_source = slot_lists(
        cols, live, place, slots, n_row * bps, late_from, bps
    )
    sums = early_product(mats, pieces[:-1], rows, index, slots)
    halves = []
    for part in range(2):
        halves.append(
            late_product(
                mats, pieces[-1], sums[part], rows, late_count, late_entry, late_source, slots, part
            )
        )
    away, kept = halves
    chunk = rpc * bs
    arrived = lax.ppermute(away, "col", to_c)

    def part_of(value, at):
        return value[at * chunk : (at + 1) * chunk]

    moving = None
    for at in range(ny - 1):
        total = part_of(kept, at).astype(F32) + part_of(arrived, at).astype(F32)
        if moving is not None:
            total = total + moving.astype(F32)
        moving = lax.ppermute(total.astype(BF16), "col", to_y)
    total = part_of(kept, ny - 1).astype(F32) + part_of(arrived, ny - 1).astype(F32)
    if moving is not None:
        total = total + moving.astype(F32)
    aggregated = total.astype(BF16)

    preact = jnp.dot(aggregated, weight, preferred_element_type=F32) + bias
    sigmoid_pre = jax.nn.sigmoid(preact)
    outputs_here = (preact * sigmoid_pre).astype(BF16)
    derivative = sigmoid_pre * (1.0 + preact * (1.0 - sigmoid_pre))
    grad_pre = (upstream.astype(F32) * derivative).astype(BF16)
    grad_agg = jnp.einsum("ng,fg->nf", grad_pre, weight, preferred_element_type=F32).astype(BF16)

    grads = []
    moving = grad_agg
    for v in range(ny):
        across = moving
        grads.append(across)
        for _ in range(1, nc):
            across = lax.ppermute(across, "col", to_c)
            grads.append(across)
        if v < ny - 1:
            moving = lax.ppermute(moving, "col", to_y)

    weight_part = jnp.einsum("nf,ng->fg", aggregated, grad_pre, preferred_element_type=F32)
    bias_part = jnp.sum(grad_pre.astype(F32), axis=0)
    unit = n_col * 8
    packed = jnp.concatenate(
        [weight_part, jnp.broadcast_to(bias_part[None, :], (unit, width))], axis=0
    )
    packed = reduce_small(packed, n_row, n_col)
    weight_grad, bias_grad = packed[:width], packed[width]

    def contribution(j, t):
        return backward_product(mats, grads, lists, ((j * nx + t) * bps,), bps, slots)[0]

    moving = None
    for j in list(range(1, nz)) + [0]:
        across = None
        for t in range(1, nx):
            value = contribution(j, t)
            if across is not None:
                value = (value.astype(F32) + across.astype(F32)).astype(BF16)
            across = lax.ppermute(value, "row", to_x)
        total = contribution(j, 0).astype(F32)
        if across is not None:
            total = total + across.astype(F32)
        if moving is not None:
            total = total + moving.astype(F32)
        total = total.astype(BF16)
        if j:
            moving = lax.ppermute(total, "row", to_z)
    return outputs_here, total, weight_grad, bias_grad


def pick(parts, at):
    return lax.dynamic_index_in_dim(parts, at, 0, keepdims=False)


def reduce_small(packed, n_row, n_col):
    _, width = packed.shape
    ny, nc = split_col(n_col)
    me_col = lax.axis_index("col")
    y, c = me_col // nc, me_col % nc
    to_y, to_c = shift_major(ny, nc, 1), shift_minor(ny, nc, 1)

    def scatter(value, n, me, pairs):
        parts = value.reshape(n, value.shape[0] // n, width)
        moving = pick(parts, (me - 1) % n)
        for s in range(2, n + 1):
            moving = lax.ppermute(moving, "col", pairs) + pick(parts, (me - s) % n)
        return moving

    def gather(value, n, me, pairs):
        out = jnp.zeros((n,) + value.shape, value.dtype)
        for s in range(n):
            out = lax.dynamic_update_index_in_dim(out, value, (me - s) % n, 0)
            if s < n - 1:
                value = lax.ppermute(value, "col", pairs)
        return out.reshape(n * value.shape[0], width)

    total = scatter(packed, nc, c, to_c)
    total = scatter(total, ny, y, to_y)
    step = 1
    while step < n_row:
        other = lax.ppermute(total, "row", [(i, i ^ step) for i in range(n_row)])
        total = total + other
        step *= 2
    total = gather(total, ny, y, to_y)
    return gather(total, nc, c, to_c)


def solution(mesh):
    n_row, n_col = mesh.shape["row"], mesh.shape["col"]
    placed = (
        P(("col", "row"), None),
        P("row", "col", None, None, None),
        P("row", "col", None),
        P("row", "col"),
        P(),
        P(),
        P(("row", "col"), None),
    )

    def body(*args):
        return local(n_row, n_col, *args)

    return jax.shard_map(
        body,
        mesh=mesh,
        in_specs=placed,
        out_specs=(P(("row", "col"), None), P(("col", "row"), None), P(), P()),
        check_vma=False,
    )
```
